768 devices in a mesh: dp: 24 (over z, core), tensor: 8 (over y), pipe: 4 (over x).
Axes of the slice: x: 4, y: 8, z: 12, core: 2. Of those that a mesh axis runs over, the one named last changes fastest.
Arguments:
- normed: bfloat16 [4, 10752, 16384], P('pipe', 'dp', 'tensor'), may hold values from -0.625 to 0.625
- w_value: bfloat16 [4, 16384, 1024], P('pipe', 'tensor'), may hold values from -0.5 to 0.5
- grad_value: bfloat16 [4, 10752, 1024], P('pipe', 'dp'), may hold values from -655360 to 655360
- assistant_mask: int32 [24, 4, 8192], P('dp'), may hold values from 0 to 1, as said below
Outputs:
- value_weight_grad: float32 [4, 8, 2064, 1024], P('pipe', 'tensor', 'dp')
- passed_grad: bfloat16 [4, 10752, 16384], P('pipe', 'dp', 'tensor')
The draws below stay inside these ranges and needn't reach their ends.
Inputs may be any that keep to these rules, and one draw needn't show every extreme that they name: `assistant_mask`: assistant tokens come in runs of whole turns; every packed sequence holds at least one assistant token.
All inputs are finite; a program needn't handle non-finite values.
Results may differ from the reference program's by a relative error of at most 0.015.
Values may be sent and summed in bfloat16 or wider, within the bound.
No kernel may reach another device: no remote copies, remote signals or barrier semaphores. Data moves between devices by JAX's collectives and lax.ppermute only.
A program may use at most 64 MiB of HBM per device.

```python
import jax
import jax.numpy as jnp
from jax import lax

D = 16384
HEAD = 128
KV_HEADS = 8
TOK = 448
LEN = 8192
MICRO = 4
TOKENS = 10752
ROWS_PAD = 2064
N_DP = 24
N_TENSOR = 8
N_PIPE = 4


def draw_assistant_mask(key, part):
    span = max(LEN // 128, 1)
    turns = LEN // span
    draws = jax.random.randint(key, (N_DP, MICRO, turns), 0, 1000)
    replica = jnp.arange(N_DP, dtype=jnp.int32)[:, None, None]
    limit = 200 + 400 * replica // max(N_DP - 1, 1)
    active = (draws < limit).astype(jnp.int32)
    active = active.at[:, :, turns - 1].set(1)
    return jnp.repeat(active, span, axis=2).astype(jnp.int32)


def steps_of(key, shape, split, smallest, top_value):
    def one(position, parts):
        heights = jax.random.uniform(jax.random.fold_in(jax.random.fold_in(key, 6), position), (parts,), jnp.float32, smallest / len(split), top_value / len(split))
        return jnp.repeat(jnp.exp(heights), shape[position] // parts).reshape((-1,) + (1,) * (len(shape) - position - 1))

    level = one(*split[0])
    for cut in split[1:]:
        level = level * one(*cut)
    return level


def scatter_about(stream_key, dims, width, reach, cuts=(), kind=jnp.bfloat16):
    level = steps_of(stream_key, dims, cuts, -0.22, 0.18) if cuts else 1.0
    array = jax.random.normal(stream_key, dims, jnp.float32) * width * level
    return jnp.minimum(jnp.maximum(array, -reach), reach).astype(kind)


def setup_inputs(seed: int = 0) -> dict:
    streams_of = jax.random.split(jax.random.key(seed), 5)
    return {
        "normed": scatter_about(streams_of[0], (N_PIPE, TOKENS, D), 0.1, 0.625, ((0, 4), (1, 24), (2, 8))),
        "w_value": scatter_about(streams_of[1], (N_PIPE, D, KV_HEADS * HEAD), HEAD ** -0.5, 0.5, ((0, 4), (1, 8))),
        "grad_value": scatter_about(streams_of[2], (N_PIPE, TOKENS, KV_HEADS * HEAD), (N_DP * MICRO * LEN // 7), 655360.0, ((0, 4), (1, 24))),
        "assistant_mask": draw_assistant_mask(jax.random.fold_in(streams_of[4], 71), 0),
    }


def reference(normed, w_value, grad_value, assistant_mask):
    mask_sum = jnp.sum(assistant_mask, dtype=jnp.int32)
    divisor = mask_sum.astype(jnp.float32)
    block_rows = D // N_TENSOR
    weight_grads = []
    input_grads = []
    for section in range(N_PIPE):
        inputs = normed[section]
        weight = w_value[section]
        upstream = grad_value[section]
        input_blocks = inputs.reshape(N_DP, TOK, D)
        upstream_blocks = upstream.reshape(N_DP, TOK, KV_HEADS * HEAD)

        def accumulate(carry, pair):
            block_in, block_up = pair
            term = jnp.dot(block_in.T, block_up, preferred_element_type=jnp.float32).astype(jnp.bfloat16)
            term = lax.optimization_barrier(term)
            return carry + term.astype(jnp.float32), None

        weight_sum, _ = lax.scan(accumulate, jnp.zeros((D, KV_HEADS * HEAD), jnp.float32), (input_blocks, upstream_blocks))
        scaled = (weight_sum / divisor).reshape(N_TENSOR, block_rows, KV_HEADS * HEAD)
        weight_grads.append(jnp.pad(scaled, ((0, 0), (0, ROWS_PAD - block_rows), (0, 0))))
        input_sum = jnp.zeros((TOKENS, D), jnp.float32)
        for head in range(KV_HEADS):
            piece_up = upstream[:, head * HEAD:(head + 1) * HEAD]
            piece_w = weight[:, head * HEAD:(head + 1) * HEAD]
            part = jnp.dot(piece_up, piece_w.T, preferred_element_type=jnp.float32).astype(jnp.bfloat16)
            part = lax.optimization_barrier(part)
            input_sum = input_sum + part.astype(jnp.float32)
        input_grads.append((input_sum / divisor).astype(jnp.bfloat16))
    passed = input_grads[1:] + [jnp.zeros((TOKENS, D), jnp.bfloat16)]
    return jnp.stack(weight_grads), jnp.stack(passed)
```

```python
import functools

import jax
import jax.numpy as jnp
from jax import lax
from jax.experimental import pallas as pl
from jax.experimental.pallas import tpu as pltpu
from jax.sharding import PartitionSpec as P

DIGITS = 6


def from_behind(block, axis, distance):
    devices = range(lax.axis_size(axis))
    route = [(i - distance, i) for i in devices if i - distance in devices]
    return lax.ppermute(block, axis, route)


def term_kernel(n, rows, mask_ref, normed_ref, grad_ref, out_ref, spread_ref):
    tokens, width = normed_ref.shape
    pieces = []
    for d in range(n):
        low, high = d * rows, min((d + 1) * rows, width)
        pieces += [normed_ref[:, low:high], jnp.zeros((tokens, rows + 1 - (high - low)), jnp.bfloat16)]
    spread_ref[...] = jnp.concatenate(pieces, axis=1)
    count = jnp.sum(mask_ref[...])
    lane = lax.broadcasted_iota(jnp.int32, (1, out_ref.shape[1]), 1)
    digit = jnp.bitwise_and(jnp.right_shift(count, 3 * jnp.minimum(lane, DIGITS)), 7).astype(jnp.float32)
    digit = jnp.where(lane < DIGITS, digit, 0.0)
    step = 256
    for m in range(0, out_ref.shape[0], step):
        size = min(step, out_ref.shape[0] - m)
        tile = lax.dot_general(
            spread_ref[:, m : m + size], grad_ref[...], (((0,), (0,)), ((), ())), preferred_element_type=jnp.float32
        )
        row = lax.broadcasted_iota(jnp.int32, (size, 1), 0) + (m + 1)
        out_ref[m : m + size, :] = jnp.where(row % (rows + 1) == 0, digit, tile).astype(jnp.bfloat16)


def terms(inputs, upstream, mask, n, rows):
    total = n * (rows + 1)
    return pl.pallas_call(
        functools.partial(term_kernel, n, rows),
        out_shape=jax.ShapeDtypeStruct((total, upstream.shape[1]), jnp.bfloat16),
        in_specs=[pl.BlockSpec(memory_space=pltpu.VMEM)] * 3,
        out_specs=pl.BlockSpec(memory_space=pltpu.VMEM),
        scratch_shapes=[pltpu.VMEM((inputs.shape[0], total), jnp.bfloat16)],
        name="terms",
        cost_estimate=pl.CostEstimate(flops=2 * inputs.size * upstream.shape[1], bytes_accessed=8 << 20, transcendentals=0),
    )(mask, inputs, upstream)


def local(normed, w_value, grad_value, assistant_mask):
    inputs = normed[0]
    weight = w_value[0]
    upstream = grad_value[0]
    n = lax.axis_size("dp")
    rows = -(-inputs.shape[1] // n)

    total = lax.dot_general(upstream, weight, (((1,), (1,)), ((), ())), preferred_element_type=jnp.float32).astype(jnp.bfloat16)
    passed = from_behind(total, "pipe", -1)
    upstream, inputs, _ = lax.optimization_barrier((upstream, inputs, total))
    mask = assistant_mask.reshape(-1, 128)
    term = terms(inputs, upstream, mask, n, rows)
    mine = lax.psum_scatter(term, "dp", scatter_dimension=0, tiled=True).astype(jnp.float32)
    scale = 8 ** jnp.arange(DIGITS, dtype=jnp.int32)
    divisor = jnp.sum(mine[rows, :DIGITS] * scale.astype(jnp.float32))
    weight_grad = mine[:rows] / divisor
    input_grad = (passed.astype(jnp.float32) / divisor).astype(jnp.bfloat16)
    return (weight_grad[None, None], input_grad[None])


def solution(mesh):
    return jax.shard_map(
        local,
        mesh=mesh,
        in_specs=(
            P("pipe", "dp", "tensor"),
            P("pipe", "tensor", None),
            P("pipe", "dp", None),
            P("dp", None, None),
        ),
        out_specs=(P("pipe", "tensor", "dp", None), P("pipe", "dp", "tensor")),
        check_vma=False,
    )
```

```python
import functools

import jax
import jax.numpy as jnp
from jax import lax
from jax.experimental import pallas as pl
from jax.experimental.pallas import tpu as pltpu
from jax.sharding import PartitionSpec as P

DIGITS = 6
EXTRA = 16
VM = pl.BlockSpec(memory_space=pltpu.VMEM)


def from_behind(block, axis, distance):
    devices = range(lax.axis_size(axis))
    route = [(i - distance, i) for i in devices if i - distance in devices]
    return lax.ppermute(block, axis, route)


def pack_kernel(chips, rows, core_ref, mask_ref, normed_ref, grad_ref, own_ref, other_ref):
    tokens, width = normed_ref.shape
    lanes = own_ref.shape[1]
    count = jnp.sum(mask_ref[...])
    lane = lax.broadcasted_iota(jnp.int32, (EXTRA, grad_ref.shape[1]), 1)
    row = lax.broadcasted_iota(jnp.int32, (EXTRA, grad_ref.shape[1]), 0)
    digit = jnp.bitwise_and(jnp.right_shift(count, 3 * jnp.minimum(lane, DIGITS)), 7)
    digit = jnp.where((lane < DIGITS) & (row == 0), digit, 0).astype(jnp.float32).astype(jnp.bfloat16)
    at = lax.broadcasted_iota(jnp.int32, (EXTRA, lanes), 1)
    first = lax.broadcasted_iota(jnp.int32, (EXTRA, lanes), 0) == 0
    marks = first & (at % (rows + 1) == rows) & (at < chips * (rows + 1))
    marks = jnp.where(marks, 1.0, 0.0).astype(jnp.bfloat16)
    other_ref[:tokens, lanes:] = grad_ref[...]
    other_ref[tokens:, lanes:] = digit
    for ref in (own_ref, other_ref):
        ref[tokens:, :lanes] = marks

    def spread(parity, ref):
        pieces = []
        for j in range(chips):
            low = (2 * j + parity) * rows
            high = min(low + rows, width)
            pieces += [normed_ref[:, low:high], jnp.zeros((tokens, rows + 1 - (high - low)), jnp.bfloat16)]
        pieces.append(jnp.zeros((tokens, lanes - chips * (rows + 1)), jnp.bfloat16))
        ref[:tokens, :lanes] = jnp.concatenate(pieces, axis=1)

    @pl.when(core_ref[0] == 0)
    def _():
        spread(0, own_ref)
        spread(1, other_ref)

    @pl.when(core_ref[0] != 0)
    def _():
        spread(1, own_ref)
        spread(0, other_ref)


def pack(core, mask, inputs, upstream, chips, rows):
    lanes = -(-chips * (rows + 1) // 128) * 128
    height = inputs.shape[0] + EXTRA
    return pl.pallas_call(
        functools.partial(pack_kernel, chips, rows),
        out_shape=(
            jax.ShapeDtypeStruct((height, lanes), jnp.bfloat16),
            jax.ShapeDtypeStruct((height, lanes + upstream.shape[1]), jnp.bfloat16),
        ),
        in_specs=[pl.BlockSpec(memory_space=pltpu.SMEM)] + [VM] * 3,
        out_specs=(VM, VM),
        name="pack",
        compiler_params=pltpu.CompilerParams(vmem_limit_bytes=60 << 20),
        cost_estimate=pl.CostEstimate(flops=0, bytes_accessed=7 << 20, transcendentals=0),
    )(core, mask, inputs, upstream)


def term_kernel(own_ref, other_ref, partner_ref, out_ref):
    lanes = own_ref.shape[1]
    step = 256
    for m in range(0, out_ref.shape[0], step):
        size = min(step, out_ref.shape[0] - m)
        tile = sum(
            lax.dot_general(
                left[:, m : m + size], right[:, lanes:], (((0,), (0,)), ((), ())), preferred_element_type=jnp.float32
            )
            for left, right in ((own_ref, other_ref), (partner_ref, partner_ref))
        )
        out_ref[m : m + size, :] = tile.astype(jnp.bfloat16)


def terms(own, other, partner, rows, width):
    return pl.pallas_call(
        term_kernel,
        out_shape=jax.ShapeDtypeStruct((rows, width), jnp.bfloat16),
        in_specs=[VM] * 3,
        out_specs=VM,
        name="terms",
        compiler_params=pltpu.CompilerParams(vmem_limit_bytes=20 << 20),
        cost_estimate=pl.CostEstimate(flops=4 * own.shape[0] * rows * width, bytes_accessed=6 << 20, transcendentals=0),
    )(own, other, partner)


def product_kernel(grad_ref, weight_ref, out_ref, held_ref, arrived):
    parts, step = held_ref.shape[0], held_ref.shape[1]
    copies = [
        pltpu.make_async_copy(weight_ref.at[pl.ds(i * step, step)], held_ref.at[i], arrived.at[i]) for i in range(parts)
    ]
    for copy in copies:
        copy.start()
    for i, copy in enumerate(copies):
        copy.wait()
        out_ref[:, i * step : (i + 1) * step] = lax.dot_general(
            grad_ref[...], held_ref[i], (((1,), (1,)), ((), ())), preferred_element_type=jnp.float32
        ).astype(jnp.bfloat16)


def product(grad, weight):
    parts = 4
    step = weight.shape[0] // parts
    return pl.pallas_call(
        product_kernel,
        out_shape=jax.ShapeDtypeStruct((grad.shape[0], weight.shape[0]), jnp.bfloat16),
        in_specs=[VM, pl.BlockSpec(memory_space=pltpu.HBM)],
        out_specs=VM,
        scratch_shapes=[pltpu.VMEM((parts, step, weight.shape[1]), jnp.bfloat16), pltpu.SemaphoreType.DMA((parts,))],
        name="product",
        compiler_params=pltpu.CompilerParams(vmem_limit_bytes=55 << 20),
        cost_estimate=pl.CostEstimate(flops=2 * grad.size * weight.shape[0], bytes_accessed=7 << 20, transcendentals=0),
    )(grad, weight)


def finish_kernel(mine_ref, passed_ref, weight_out_ref, passed_out_ref, held_ref, done):
    rows = weight_out_ref.shape[0]
    digits = mine_ref[rows : rows + 1, :128].astype(jnp.float32)
    lane = lax.broadcasted_iota(jnp.int32, (1, 128), 1)
    scale = jnp.where(lane < DIGITS, jnp.left_shift(1, 3 * jnp.minimum(lane, DIGITS)), 0).astype(jnp.float32)
    inverse = 1.0 / jnp.sum(digits * scale)
    parts = held_ref.shape[0]
    step = passed_ref.shape[0] // parts
    copies = []
    for i in range(parts):
        held_ref[i] = (passed_ref[i * step : (i + 1) * step, :].astype(jnp.float32) * inverse).astype(jnp.bfloat16)
        copies.append(pltpu.make_async_copy(held_ref.at[i], passed_out_ref.at[pl.ds(i * step, step)], done.at[i]))
        copies[-1].start()
    for q in range(weight_out_ref.shape[1]):
        weight_out_ref[:, q, :] = mine_ref[:rows, 128 * q : 128 * (q + 1)].astype(jnp.float32) * inverse
    for copy in copies:
        copy.wait()


def finish(mine, passed):
    rows, parts = mine.shape[0] - 1, 4
    return pl.pallas_call(
        finish_kernel,
        out_shape=(
            jax.ShapeDtypeStruct((rows, mine.shape[1] // 128, 128), jnp.float32),
            jax.ShapeDtypeStruct(passed.shape, jnp.bfloat16),
        ),
        in_specs=[VM, VM],
        out_specs=(VM, pl.BlockSpec(memory_space=pltpu.HBM)),
        scratch_shapes=[
            pltpu.VMEM((parts, passed.shape[0] // parts, passed.shape[1]), jnp.bfloat16),
            pltpu.SemaphoreType.DMA((parts,)),
        ],
        name="finish",
        compiler_params=pltpu.CompilerParams(vmem_limit_bytes=20 << 20),
    )(mine, passed)


def local(normed, w_value, grad_value, assistant_mask):
    inputs = normed[0]
    weight = w_value[0]
    upstream = grad_value[0]
    n = lax.axis_size("dp")
    chips = n // 2
    rows = -(-inputs.shape[1] // n)
    core = lax.rem(lax.axis_index("dp"), 2).reshape(1)

    own, other = pack(core, assistant_mask[0], inputs, upstream, chips, rows)
    partner = lax.ppermute(other, "dp", [(i, i ^ 1) for i in range(n)])
    upstream, _ = lax.optimization_barrier((upstream, other))
    passed = from_behind(product(upstream, weight), "pipe", -1)
    term = terms(own, other, partner, chips * (rows + 1), upstream.shape[1])
    parity = [[2 * z + c for z in range(chips)] for c in range(2)]
    mine = lax.psum_scatter(term, "dp", scatter_dimension=0, tiled=True, axis_index_groups=parity)
    weight_grad, input_grad = finish(mine, passed)
    return (weight_grad.reshape(1, 1, rows, -1), input_grad[None])


def solution(mesh):
    return jax.shard_map(
        local,
        mesh=mesh,
        in_specs=(
            P("pipe", "dp", "tensor"),
            P("pipe", "tensor", None),
            P("pipe", "dp", None),
            P("dp", None, None),
        ),
        out_specs=(P("pipe", "tensor", "dp", None), P("pipe", "dp", "tensor")),
        check_vma=False,
    )
```

```python
import functools

import jax
import jax.numpy as jnp
from jax import lax
from jax.experimental import pallas as pl
from jax.experimental.pallas import tpu as pltpu
from jax.sharding import PartitionSpec as P

DIGITS = 6
EXTRA = 16
PARTS = 4
VM = pl.BlockSpec(memory_space=pltpu.VMEM)
ANY = pl.BlockSpec(memory_space=pl.ANY)


def from_behind(block, axis, distance):
    devices = range(lax.axis_size(axis))
    route = [(i - distance, i) for i in devices if i - distance in devices]
    return lax.ppermute(block, axis, route)


def pack_kernel(
    chips, rows, core_ref, mask_ref, normed_ref, grad_ref, own_ref, other_ref, mask, normed, own, other, arrived, left
):
    tokens, width = normed.shape
    lanes, columns = own.shape[1], grad_ref.shape[1]
    parts = PARTS
    step = tokens // parts
    loads = [pltpu.make_async_copy(mask_ref, mask, arrived.at[2 * parts])]
    for i in range(parts):
        at = pl.ds(i * step, step)
        loads.append(pltpu.make_async_copy(normed_ref.at[at], normed.at[at], arrived.at[2 * i]))
        loads.append(pltpu.make_async_copy(grad_ref.at[at], other.at[at, pl.ds(lanes, columns)], arrived.at[2 * i + 1]))
    for load in loads:
        load.start()

    loads[0].wait()
    count = jnp.sum(mask[...])
    lane = lax.broadcasted_iota(jnp.int32, (EXTRA, columns), 1)
    row = lax.broadcasted_iota(jnp.int32, (EXTRA, columns), 0)
    digit = jnp.bitwise_and(jnp.right_shift(count, 3 * jnp.minimum(lane, DIGITS)), 7)
    digit = jnp.where((lane < DIGITS) & (row == 0), digit, 0).astype(jnp.float32).astype(jnp.bfloat16)
    at = lax.broadcasted_iota(jnp.int32, (EXTRA, lanes), 1)
    first = lax.broadcasted_iota(jnp.int32, (EXTRA, lanes), 0) == 0
    marks = first & (at % (rows + 1) == rows) & (at < chips * (rows + 1))
    marks = jnp.where(marks, 1.0, 0.0).astype(jnp.bfloat16)
    other[tokens:, lanes:] = digit
    other[tokens:, :lanes] = marks
    own[tokens:, :] = marks

    def spread(low, parity, ref):
        pieces = []
        for j in range(chips):
            begin = (2 * j + parity) * rows
            end = min(begin + rows, width)
            pieces += [normed[low : low + step, begin:end], jnp.zeros((step, rows + 1 - (end - begin)), jnp.bfloat16)]
        pieces.append(jnp.zeros((step, lanes - chips * (rows + 1)), jnp.bfloat16))
        ref[low : low + step, :lanes] = jnp.concatenate(pieces, axis=1)

    stores = []
    for i in range(parts):
        loads[2 * i + 1].wait()
        loads[2 * i + 2].wait()
        for core in range(2):

            @pl.when(core_ref[0] == core)
            def _():
                spread(i * step, core, own)
                spread(i * step, 1 - core, other)

        at = pl.ds(i * step, step if i < parts - 1 else step + EXTRA)
        stores.append(pltpu.make_async_copy(other.at[at], other_ref.at[at], left.at[2 * i]))
        stores.append(pltpu.make_async_copy(own.at[at], own_ref.at[at], left.at[2 * i + 1]))
        stores[-2].start()
        stores[-1].start()
    for store in stores:
        store.wait()


def pack(core, mask, inputs, upstream, chips, rows):
    lanes = -(-chips * (rows + 1) // 128) * 128
    height = inputs.shape[0] + EXTRA
    own = jax.ShapeDtypeStruct((height, lanes), jnp.bfloat16)
    other = jax.ShapeDtypeStruct((height, lanes + upstream.shape[1]), jnp.bfloat16)
    return pl.pallas_call(
        functools.partial(pack_kernel, chips, rows),
        out_shape=(own, other),
        in_specs=[pl.BlockSpec(memory_space=pltpu.SMEM)] + [ANY] * 3,
        out_specs=(ANY, ANY),
        scratch_shapes=[
            pltpu.VMEM(mask.shape, mask.dtype),
            pltpu.VMEM(inputs.shape, inputs.dtype),
            pltpu.VMEM(own.shape, own.dtype),
            pltpu.VMEM(other.shape, other.dtype),
            pltpu.SemaphoreType.DMA((2 * PARTS + 1,)),
            pltpu.SemaphoreType.DMA((2 * PARTS,)),
        ],
        name="pack",
        compiler_params=pltpu.CompilerParams(vmem_limit_bytes=60 << 20),
        cost_estimate=pl.CostEstimate(flops=0, bytes_accessed=7 << 20, transcendentals=0),
    )(core, mask, inputs, upstream)


def term_kernel(own_ref, other_ref, partner_ref, out_ref):
    lanes = own_ref.shape[1]
    step = 256
    for m in range(0, out_ref.shape[0], step):
        size = min(step, out_ref.shape[0] - m)
        tile = sum(
            lax.dot_general(
                left[:, m : m + size], right[:, lanes:], (((0,), (0,)), ((), ())), preferred_element_type=jnp.float32
            )
            for left, right in ((own_ref, other_ref), (partner_ref, partner_ref))
        )
        out_ref[m : m + size, :] = tile.astype(jnp.bfloat16)


def terms(own, other, partner, rows, width):
    return pl.pallas_call(
        term_kernel,
        out_shape=jax.ShapeDtypeStruct((rows, width), jnp.bfloat16),
        in_specs=[VM] * 3,
        out_specs=VM,
        name="terms",
        compiler_params=pltpu.CompilerParams(vmem_limit_bytes=20 << 20),
        cost_estimate=pl.CostEstimate(flops=4 * own.shape[0] * rows * width, bytes_accessed=6 << 20, transcendentals=0),
    )(own, other, partner)


def product_kernel(grad_ref, weight_ref, out_ref, grad, weight, out, arrived, left):
    parts, step = weight.shape[0], weight.shape[1]
    loads = [pltpu.make_async_copy(grad_ref, grad, arrived.at[parts])]
    for i in range(parts):
        loads.append(pltpu.make_async_copy(weight_ref.at[pl.ds(i * step, step)], weight.at[i], arrived.at[i]))
    for load in loads:
        load.start()
    loads[0].wait()
    stores = []
    for i in range(parts):
        loads[i + 1].wait()
        out[i] = lax.dot_general(
            grad[...], weight[i], (((1,), (1,)), ((), ())), preferred_element_type=jnp.float32
        ).astype(jnp.bfloat16)
        stores.append(pltpu.make_async_copy(out.at[i], out_ref.at[:, pl.ds(i * step, step)], left.at[i]))
        stores[-1].start()
    for store in stores:
        store.wait()


def product(grad, weight):
    tokens, width = grad.shape[0], weight.shape[0]
    step = width // PARTS
    return pl.pallas_call(
        product_kernel,
        out_shape=jax.ShapeDtypeStruct((tokens, width), jnp.bfloat16),
        in_specs=[ANY, ANY],
        out_specs=ANY,
        scratch_shapes=[
            pltpu.VMEM(grad.shape, grad.dtype),
            pltpu.VMEM((PARTS, step, weight.shape[1]), weight.dtype),
            pltpu.VMEM((PARTS, tokens, step), jnp.bfloat16),
            pltpu.SemaphoreType.DMA((PARTS + 1,)),
            pltpu.SemaphoreType.DMA((PARTS,)),
        ],
        name="product",
        compiler_params=pltpu.CompilerParams(vmem_limit_bytes=55 << 20),
        cost_estimate=pl.CostEstimate(flops=2 * grad.size * width, bytes_accessed=7 << 20, transcendentals=0),
    )(grad, weight)


def finish_kernel(mine_ref, passed_ref, weight_out_ref, passed_out_ref, mine, passed, weight_out, arrived, left):
    rows = weight_out_ref.shape[0]
    parts = PARTS
    step = passed.shape[0] // parts
    loads = [pltpu.make_async_copy(mine_ref, mine, arrived.at[parts])]
    for i in range(parts):
        at = pl.ds(i * step, step)
        loads.append(pltpu.make_async_copy(passed_ref.at[at], passed.at[at], arrived.at[i]))
    for load in loads:
        load.start()
    loads[0].wait()
    digits = mine[rows : rows + 1, :128].astype(jnp.float32)
    lane = lax.broadcasted_iota(jnp.int32, (1, 128), 1)
    scale = jnp.where(lane < DIGITS, jnp.left_shift(1, 3 * jnp.minimum(lane, DIGITS)), 0).astype(jnp.float32)
    inverse = 1.0 / jnp.sum(digits * scale)
    for q in range(weight_out_ref.shape[1]):
        weight_out[:, q, :] = mine[:rows, 128 * q : 128 * (q + 1)].astype(jnp.float32) * inverse
    stores = [pltpu.make_async_copy(weight_out, weight_out_ref, left.at[parts])]
    stores[0].start()
    for i in range(parts):
        at = pl.ds(i * step, step)
        loads[i + 1].wait()
        passed[at, :] = (passed[at, :].astype(jnp.float32) * inverse).astype(jnp.bfloat16)
        stores.append(pltpu.make_async_copy(passed.at[at], passed_out_ref.at[at], left.at[i]))
        stores[-1].start()
    for store in stores:
        store.wait()


def finish(mine, passed):
    weight_out = jax.ShapeDtypeStruct((mine.shape[0] - 1, mine.shape[1] // 128, 128), jnp.float32)
    return pl.pallas_call(
        finish_kernel,
        out_shape=(weight_out, jax.ShapeDtypeStruct(passed.shape, jnp.bfloat16)),
        in_specs=[ANY, ANY],
        out_specs=(ANY, ANY),
        scratch_shapes=[
            pltpu.VMEM(mine.shape, mine.dtype),
            pltpu.VMEM(passed.shape, passed.dtype),
            pltpu.VMEM(weight_out.shape, weight_out.dtype),
            pltpu.SemaphoreType.DMA((PARTS + 1,)),
            pltpu.SemaphoreType.DMA((PARTS + 1,)),
        ],
        name="finish",
        compiler_params=pltpu.CompilerParams(vmem_limit_bytes=20 << 20),
    )(mine, passed)


def local(normed, w_value, grad_value, assistant_mask):
    inputs = normed[0]
    weight = w_value[0]
    upstream = grad_value[0]
    n = lax.axis_size("dp")
    chips = n // 2
    rows = -(-inputs.shape[1] // n)
    core = lax.rem(lax.axis_index("dp"), 2).reshape(1)

    own, other = pack(core, assistant_mask[0], inputs, upstream, chips, rows)
    partner = lax.ppermute(other, "dp", [(i, i ^ 1) for i in range(n)])
    upstream, _ = lax.optimization_barrier((upstream, other))
    passed = from_behind(product(upstream, weight), "pipe", -1)
    term = terms(own, other, partner, chips * (rows + 1), upstream.shape[1])
    parity = [[2 * z + c for z in range(chips)] for c in range(2)]
    mine = lax.psum_scatter(term, "dp", scatter_dimension=0, tiled=True, axis_index_groups=parity)
    weight_grad, input_grad = finish(mine, passed)
    return (weight_grad.reshape(1, 1, rows, -1), input_grad[None])


def solution(mesh):
    return jax.shard_map(
        local,
        mesh=mesh,
        in_specs=(
            P("pipe", "dp", "tensor"),
            P("pipe", "tensor", None),
            P("pipe", "dp", None),
            P("dp", None, None),
        ),
        out_specs=(P("pipe", "tensor", "dp", None), P("pipe", "dp", "tensor")),
        check_vma=False,
    )
```

```python
import functools

import jax
import jax.numpy as jnp
from jax import lax
from jax.experimental import pallas as pl
from jax.experimental.pallas import tpu as pltpu
from jax.sharding import PartitionSpec as P

DIGITS = 6
EXTRA = 16
TILE = 256
PARTS = 4
VM = pl.BlockSpec(memory_space=pltpu.VMEM)
ANY = pl.BlockSpec(memory_space=pl.ANY)


def from_behind(block, axis, distance):
    devices = range(lax.axis_size(axis))
    route = [(i - distance, i) for i in devices if i - distance in devices]
    return lax.ppermute(block, axis, route)


def front_kernel(
    chips, rows, core_ref, mask_ref, normed_ref, grad_ref, weight_ref, own_ref, other_ref, low_ref, high_ref,
    mask, normed, grad, weight, packs, product, arrived, left,
):
    tokens, width = normed.shape
    lanes, columns = own_ref.shape[1], grad_ref.shape[1]
    step, slab = tokens // PARTS, width // PARTS
    loads = [
        pltpu.make_async_copy(grad_ref, grad.at[pl.ds(0, tokens)], arrived.at[0]),
        pltpu.make_async_copy(mask_ref, mask, arrived.at[1]),
    ]
    for i in range(PARTS):
        at = pl.ds(i * step, step)
        loads.append(pltpu.make_async_copy(weight_ref.at[pl.ds(i * slab, slab)], weight.at[i], arrived.at[2 * i + 2]))
        loads.append(pltpu.make_async_copy(normed_ref.at[at], normed.at[at], arrived.at[2 * i + 3]))
    for load in loads:
        load.start()

    at = lax.broadcasted_iota(jnp.int32, (EXTRA, lanes), 1)
    first = lax.broadcasted_iota(jnp.int32, (EXTRA, lanes), 0) == 0
    marks = first & (at % (rows + 1) == rows) & (at < chips * (rows + 1))
    marks = jnp.where(marks, 1.0, 0.0).astype(jnp.bfloat16)
    for parity in range(2):
        packs[parity, tokens:, :] = marks
    lane = lax.broadcasted_iota(jnp.int32, (EXTRA, columns), 1)
    row = lax.broadcasted_iota(jnp.int32, (EXTRA, columns), 0)
    loads[0].wait()
    loads[1].wait()
    count = jnp.sum(mask[...])
    digit = jnp.bitwise_and(jnp.right_shift(count, 3 * jnp.minimum(lane, DIGITS)), 7)
    digit = jnp.where((lane < DIGITS) & (row == 0), digit, 0).astype(jnp.float32).astype(jnp.bfloat16)
    grad[tokens:, :] = digit
    core = core_ref[0]
    stores = [pltpu.make_async_copy(grad, other_ref.at[:, pl.ds(lanes, columns)], left.at[0])]
    stores[0].start()

    for i in range(PARTS):
        loads[2 * i + 2].wait()
        loads[2 * i + 3].wait()
        product[i] = lax.dot_general(
            grad[:tokens, :], weight[i], (((1,), (1,)), ((), ())), preferred_element_type=jnp.float32
        ).astype(jnp.bfloat16)
        for parity in range(2):
            pieces = []
            for j in range(chips):
                begin = (2 * j + parity) * rows
                end = min(begin + rows, width)
                pieces.append(normed[i * step : (i + 1) * step, begin:end])
                pieces.append(jnp.zeros((step, rows + 1 - (end - begin)), jnp.bfloat16))
            pieces.append(jnp.zeros((step, lanes - chips * (rows + 1)), jnp.bfloat16))
            packs[parity, i * step : (i + 1) * step, :] = jnp.concatenate(pieces, axis=1)
        at = pl.ds(i * step, step if i < PARTS - 1 else step + EXTRA)
        half = (low_ref, high_ref)[2 * i // PARTS]
        place = pl.ds(i % (PARTS // 2) * slab, slab)
        stores.append(pltpu.make_async_copy(packs.at[1 - core, at], other_ref.at[at, pl.ds(0, lanes)], left.at[3 * i + 1]))
        stores.append(pltpu.make_async_copy(product.at[i], half.at[:, place], left.at[3 * i + 2]))
        stores.append(pltpu.make_async_copy(packs.at[core, at], own_ref.at[at], left.at[3 * i + 3]))
        for store in stores[-3:]:
            store.start()
    for store in stores:
        store.wait()


def front(core, mask, inputs, upstream, weight, chips, rows):
    lanes = -(-chips * (rows + 1) // 128) * 128
    (tokens, width), columns = inputs.shape, upstream.shape[1]
    height = tokens + EXTRA
    bf16 = jnp.bfloat16
    half = jax.ShapeDtypeStruct((tokens, width // 2), bf16)
    return pl.pallas_call(
        functools.partial(front_kernel, chips, rows),
        out_shape=(
            jax.ShapeDtypeStruct((height, lanes), bf16),
            jax.ShapeDtypeStruct((height, lanes + columns), bf16),
            half,
            half,
        ),
        in_specs=[pl.BlockSpec(memory_space=pltpu.SMEM)] + [ANY] * 4,
        out_specs=(ANY,) * 4,
        scratch_shapes=[
            pltpu.VMEM(mask.shape, mask.dtype),
            pltpu.VMEM(inputs.shape, bf16),
            pltpu.VMEM((height, columns), bf16),
            pltpu.VMEM((PARTS, width // PARTS, columns), bf16),
            pltpu.VMEM((2, height, lanes), bf16),
            pltpu.VMEM((PARTS, tokens, width // PARTS), bf16),
            pltpu.SemaphoreType.DMA((2 * PARTS + 2,)),
            pltpu.SemaphoreType.DMA((3 * PARTS + 1,)),
        ],
        name="front",
        compiler_params=pltpu.CompilerParams(vmem_limit_bytes=60 << 20),
        cost_estimate=pl.CostEstimate(flops=2 * upstream.size * width, bytes_accessed=14 << 20, transcendentals=0),
    )(core, mask, inputs, upstream, weight)


def term_kernel(own_ref, other_ref, partner_ref, out_ref, own, grad, partner, first, out, arrived, left):
    lanes = own.shape[1]
    loads = [
        pltpu.make_async_copy(other_ref.at[:, pl.ds(lanes, grad.shape[1])], grad, arrived.at[0]),
        pltpu.make_async_copy(own_ref, own, arrived.at[1]),
        pltpu.make_async_copy(partner_ref, partner, arrived.at[2]),
    ]
    for load in loads:
        load.start()
    tiles = [(m, min(TILE, out.shape[0] - m)) for m in range(0, out.shape[0], TILE)]

    def product(left, right):
        return lax.dot_general(left, right, (((0,), (0,)), ((), ())), preferred_element_type=jnp.float32)

    loads[0].wait()
    loads[1].wait()
    for m, size in tiles:
        first[m : m + size, :] = product(own[:, m : m + size], grad[...])
    loads[2].wait()
    stores = []
    for i, (m, size) in enumerate(tiles):
        tile = first[m : m + size, :] + product(partner[:, m : m + size], partner[:, lanes:])
        out[m : m + size, :] = tile.astype(jnp.bfloat16)
        at = pl.ds(m, size)
        stores.append(pltpu.make_async_copy(out.at[at], out_ref.at[at], left.at[i]))
        stores[-1].start()
    for store in stores:
        store.wait()


def terms(own, other, partner, rows, width):
    return pl.pallas_call(
        term_kernel,
        out_shape=jax.ShapeDtypeStruct((rows, width), jnp.bfloat16),
        in_specs=[ANY] * 3,
        out_specs=ANY,
        scratch_shapes=[
            pltpu.VMEM(own.shape, own.dtype),
            pltpu.VMEM((own.shape[0], width), own.dtype),
            pltpu.VMEM(partner.shape, partner.dtype),
            pltpu.VMEM((rows, width), jnp.float32),
            pltpu.VMEM((rows, width), jnp.bfloat16),
            pltpu.SemaphoreType.DMA((3,)),
            pltpu.SemaphoreType.DMA((-(-rows // TILE),)),
        ],
        name="terms",
        compiler_params=pltpu.CompilerParams(vmem_limit_bytes=59 << 20),
        cost_estimate=pl.CostEstimate(flops=4 * own.shape[0] * rows * width, bytes_accessed=6 << 20, transcendentals=0),
    )(own, other, partner)


def finish_kernel(
    mine_ref, low_ref, high_ref, weight_out_ref, passed_out_ref, mine, passed, weight_out, arrived, left
):
    rows = weight_out_ref.shape[0]
    width = low_ref.shape[1]
    step = low_ref.shape[0] // (PARTS // 2)
    loads = [pltpu.make_async_copy(mine_ref, mine, arrived.at[PARTS])]
    places = []
    for i in range(PARTS):
        at, half = pl.ds(i // 2 * step, step), i % 2
        places.append((at, pl.ds(half * width, width)))
        loads.append(pltpu.make_async_copy((low_ref, high_ref)[half].at[at], passed.at[i], arrived.at[i]))
    for load in loads:
        load.start()
    loads[0].wait()
    digits = mine[rows : rows + 1, :128].astype(jnp.float32)
    lane = lax.broadcasted_iota(jnp.int32, (1, 128), 1)
    scale = jnp.where(lane < DIGITS, jnp.left_shift(1, 3 * jnp.minimum(lane, DIGITS)), 0).astype(jnp.float32)
    inverse = 1.0 / jnp.sum(digits * scale)
    for q in range(weight_out_ref.shape[1]):
        weight_out[:, q, :] = mine[:rows, 128 * q : 128 * (q + 1)].astype(jnp.float32) * inverse
    stores = [pltpu.make_async_copy(weight_out, weight_out_ref, left.at[PARTS])]
    stores[0].start()
    for i in range(PARTS):
        loads[i + 1].wait()
        passed[i] = (passed[i].astype(jnp.float32) * inverse).astype(jnp.bfloat16)
        stores.append(pltpu.make_async_copy(passed.at[i], passed_out_ref.at[places[i]], left.at[i]))
        stores[-1].start()
    for store in stores:
        store.wait()


def finish(mine, low, high):
    weight_out = jax.ShapeDtypeStruct((mine.shape[0] - 1, mine.shape[1] // 128, 128), jnp.float32)
    tokens, width = low.shape
    return pl.pallas_call(
        finish_kernel,
        out_shape=(weight_out, jax.ShapeDtypeStruct((tokens, 2 * width), low.dtype)),
        in_specs=[ANY] * 3,
        out_specs=(ANY, ANY),
        scratch_shapes=[
            pltpu.VMEM(mine.shape, mine.dtype),
            pltpu.VMEM((PARTS, tokens // (PARTS // 2), width), low.dtype),
            pltpu.VMEM(weight_out.shape, weight_out.dtype),
            pltpu.SemaphoreType.DMA((PARTS + 1,)),
            pltpu.SemaphoreType.DMA((PARTS + 1,)),
        ],
        name="finish",
        compiler_params=pltpu.CompilerParams(vmem_limit_bytes=20 << 20),
    )(mine, low, high)


def local(normed, w_value, grad_value, assistant_mask):
    inputs = normed[0]
    weight = w_value[0]
    upstream = grad_value[0]
    n = lax.axis_size("dp")
    chips = n // 2
    rows = -(-inputs.shape[1] // n)
    core = lax.rem(lax.axis_index("dp"), 2).reshape(1)

    own, other, low, high = front(core, assistant_mask[0], inputs, upstream, weight, chips, rows)
    partner = lax.ppermute(other, "dp", [(i, i ^ 1) for i in range(n)])
    low, high = (from_behind(half, "pipe", -1) for half in (low, high))
    term = terms(own, other, partner, chips * (rows + 1), upstream.shape[1])
    parity = [[2 * z + c for z in range(chips)] for c in range(2)]
    mine = lax.psum_scatter(term, "dp", scatter_dimension=0, tiled=True, axis_index_groups=parity)
    weight_grad, input_grad = finish(mine, low, high)
    return (weight_grad.reshape(1, 1, rows, -1), input_grad[None])


def solution(mesh):
    return jax.shard_map(
        local,
        mesh=mesh,
        in_specs=(
            P("pipe", "dp", "tensor"),
            P("pipe", "tensor", None),
            P("pipe", "dp", None),
            P("dp", None, None),
        ),
        out_specs=(P("pipe", "tensor", "dp", None), P("pipe", "dp", "tensor")),
        check_vma=False,
    )
```

```python
import functools

import jax
import jax.numpy as jnp
from jax import lax
from jax.experimental import pallas as pl
from jax.experimental.pallas import tpu as pltpu
from jax.sharding import PartitionSpec as P

DIGITS = 6
EXTRA = 16
FRONT = 60_000_000
TILE = 256
PARTS = 4
VM = pl.BlockSpec(memory_space=pltpu.VMEM)
ANY = pl.BlockSpec(memory_space=pl.ANY)


def from_behind(block, axis, distance):
    devices = range(lax.axis_size(axis))
    route = [(i - distance, i) for i in devices if i - distance in devices]
    return lax.ppermute(block, axis, route)


def front_kernel(
    chips, rows, core_ref, mask_ref, normed_ref, grad_ref, weight_ref, own_ref, own_grad_ref, other_ref, low_ref, high_ref,
    mask, normed, grad, weight, packs, made, arrived, left,
):
    tokens, width = normed.shape
    lanes, columns = own_ref.shape[1], grad_ref.shape[1]
    step, slab = tokens // PARTS, width // PARTS
    loads = [
        pltpu.make_async_copy(grad_ref, grad.at[pl.ds(0, tokens)], arrived.at[0]),
        pltpu.make_async_copy(mask_ref, mask, arrived.at[1]),
    ]
    for i in range(PARTS):
        at = pl.ds(i * step, step)
        loads.append(pltpu.make_async_copy(weight_ref.at[pl.ds(i * slab, slab)], weight.at[i], arrived.at[2 * i + 2]))
        loads.append(pltpu.make_async_copy(normed_ref.at[at], normed.at[at], arrived.at[2 * i + 3]))
    for load in loads:
        load.start()

    at = lax.broadcasted_iota(jnp.int32, (EXTRA, lanes), 1)
    first = lax.broadcasted_iota(jnp.int32, (EXTRA, lanes), 0) == 0
    marks = first & (at % (rows + 1) == rows) & (at < chips * (rows + 1))
    marks = jnp.where(marks, 1.0, 0.0).astype(jnp.bfloat16)
    for parity in range(2):
        packs[parity, tokens:, :] = marks
    lane = lax.broadcasted_iota(jnp.int32, (EXTRA, columns), 1)
    row = lax.broadcasted_iota(jnp.int32, (EXTRA, columns), 0)
    loads[0].wait()
    loads[1].wait()
    count = jnp.sum(mask[...])
    digit = jnp.bitwise_and(jnp.right_shift(count, 3 * jnp.minimum(lane, DIGITS)), 7)
    digit = jnp.where((lane < DIGITS) & (row == 0), digit, 0).astype(jnp.float32).astype(jnp.bfloat16)
    grad[tokens:, :] = digit
    core = core_ref[0]
    stores = [
        pltpu.make_async_copy(grad, other_ref.at[:, pl.ds(lanes, columns)], left.at[0]),
        pltpu.make_async_copy(grad, own_grad_ref, left.at[3 * PARTS + 1]),
    ]
    for store in stores:
        store.start()

    for i in range(PARTS):
        loads[2 * i + 2].wait()
        loads[2 * i + 3].wait()
        made[i] = lax.dot_general(
            grad[:tokens, :], weight[i], (((1,), (1,)), ((), ())), preferred_element_type=jnp.float32
        ).astype(jnp.bfloat16)
        for parity in range(2):
            pieces = []
            for j in range(chips):
                begin = (2 * j + parity) * rows
                end = min(begin + rows, width)
                pieces.append(normed[i * step : (i + 1) * step, begin:end])
                pieces.append(jnp.zeros((step, rows + 1 - (end - begin)), jnp.bfloat16))
            pieces.append(jnp.zeros((step, lanes - chips * (rows + 1)), jnp.bfloat16))
            packs[parity, i * step : (i + 1) * step, :] = jnp.concatenate(pieces, axis=1)
        at = pl.ds(i * step, step if i < PARTS - 1 else step + EXTRA)
        half = (low_ref, high_ref)[2 * i // PARTS]
        place = pl.ds(i % (PARTS // 2) * slab, slab)
        stores.append(pltpu.make_async_copy(packs.at[1 - core, at], other_ref.at[at, pl.ds(0, lanes)], left.at[3 * i + 1]))
        stores.append(pltpu.make_async_copy(made.at[i], half.at[:, place], left.at[3 * i + 2]))
        stores.append(pltpu.make_async_copy(packs.at[core, at], own_ref.at[at], left.at[3 * i + 3]))
        for store in stores[-3:]:
            store.start()
    for store in stores:
        store.wait()


def front(core, mask, inputs, upstream, weight, chips, rows):
    lanes = -(-chips * (rows + 1) // 128) * 128
    (tokens, width), columns = inputs.shape, upstream.shape[1]
    height = tokens + EXTRA
    bf16 = jnp.bfloat16
    half = jax.ShapeDtypeStruct((tokens, width // 2), bf16)
    return pl.pallas_call(
        functools.partial(front_kernel, chips, rows),
        out_shape=(
            jax.ShapeDtypeStruct((height, lanes), bf16),
            jax.ShapeDtypeStruct((height, columns), bf16),
            jax.ShapeDtypeStruct((height, lanes + columns), bf16),
            half,
            half,
        ),
        in_specs=[pl.BlockSpec(memory_space=pltpu.SMEM)] + [ANY] * 4,
        out_specs=(ANY,) * 5,
        scratch_shapes=[
            pltpu.VMEM(mask.shape, mask.dtype),
            pltpu.VMEM(inputs.shape, bf16),
            pltpu.VMEM((height, columns), bf16),
            pltpu.VMEM((PARTS, width // PARTS, columns), bf16),
            pltpu.VMEM((2, height, lanes), bf16),
            pltpu.VMEM((PARTS, tokens, width // PARTS), bf16),
            pltpu.SemaphoreType.DMA((2 * PARTS + 2,)),
            pltpu.SemaphoreType.DMA((3 * PARTS + 2,)),
        ],
        name="front",
        compiler_params=pltpu.CompilerParams(vmem_limit_bytes=FRONT),
        cost_estimate=pl.CostEstimate(flops=2 * upstream.size * width, bytes_accessed=14 << 20, transcendentals=0),
    )(core, mask, inputs, upstream, weight)


def product(left, right):
    return lax.dot_general(left, right, (((0,), (0,)), ((), ())), preferred_element_type=jnp.float32)


def own_kernel(own_ref, grad_ref, out_ref):
    for m in range(0, out_ref.shape[0], TILE):
        size = min(TILE, out_ref.shape[0] - m)
        out_ref[m : m + size, :] = product(own_ref[:, m : m + size], grad_ref[...])


def own_terms(own, grad, rows):
    width = grad.shape[1]
    return pl.pallas_call(
        own_kernel,
        out_shape=jax.ShapeDtypeStruct((rows, width), jnp.float32),
        in_specs=[VM] * 2,
        out_specs=VM,
        name="own_terms",
        compiler_params=pltpu.CompilerParams(vmem_limit_bytes=20 << 20),
        cost_estimate=pl.CostEstimate(flops=2 * own.shape[0] * rows * width, bytes_accessed=6 << 20, transcendentals=0),
    )(own, grad)


def term_kernel(partner_ref, first_ref, out_ref):
    lanes = partner_ref.shape[1] - out_ref.shape[1]
    for m in range(0, out_ref.shape[0], TILE):
        size = min(TILE, out_ref.shape[0] - m)
        tile = product(partner_ref[:, m : m + size], partner_ref[:, lanes:]) + first_ref[m : m + size, :]
        out_ref[m : m + size, :] = tile.astype(out_ref.dtype)


def terms(partner, first):
    rows, width = first.shape
    return pl.pallas_call(
        term_kernel,
        out_shape=jax.ShapeDtypeStruct((rows, width), jnp.bfloat16),
        in_specs=[VM] * 2,
        out_specs=VM,
        name="terms",
        compiler_params=pltpu.CompilerParams(vmem_limit_bytes=20 << 20),
        cost_estimate=pl.CostEstimate(
            flops=2 * partner.shape[0] * rows * width, bytes_accessed=8 << 20, transcendentals=0
        ),
    )(partner, first)


def finish_kernel(mine_ref, low_ref, high_ref, weight_out_ref, passed_out_ref, passed, weight_out, left):
    rows = weight_out_ref.shape[0]
    width = low_ref.shape[1]
    step = low_ref.shape[0] // (PARTS // 2)
    digits = mine_ref[rows : rows + 1, :128].astype(jnp.float32)
    lane = lax.broadcasted_iota(jnp.int32, (1, 128), 1)
    scale = jnp.where(lane < DIGITS, jnp.left_shift(1, 3 * jnp.minimum(lane, DIGITS)), 0).astype(jnp.float32)
    inverse = 1.0 / jnp.sum(digits * scale)
    stores = []
    for i in range(PARTS):
        low, half = i // 2 * step, i % 2
        passed[i] = ((low_ref, high_ref)[half][low : low + step, :].astype(jnp.float32) * inverse).astype(jnp.bfloat16)
        place = passed_out_ref.at[pl.ds(low, step), pl.ds(half * width, width)]
        stores.append(pltpu.make_async_copy(passed.at[i], place, left.at[i]))
        stores[-1].start()
    for q in range(weight_out_ref.shape[1]):
        weight_out[:, q, :] = mine_ref[:rows, 128 * q : 128 * (q + 1)].astype(jnp.float32) * inverse
    stores.append(pltpu.make_async_copy(weight_out, weight_out_ref, left.at[PARTS]))
    stores[-1].start()
    for store in stores:
        store.wait()


def finish(mine, low, high):
    weight_out = jax.ShapeDtypeStruct((mine.shape[0] - 1, mine.shape[1] // 128, 128), jnp.float32)
    tokens, width = low.shape
    return pl.pallas_call(
        finish_kernel,
        out_shape=(weight_out, jax.ShapeDtypeStruct((tokens, 2 * width), low.dtype)),
        in_specs=[VM] * 3,
        out_specs=(ANY, ANY),
        scratch_shapes=[
            pltpu.VMEM((PARTS, tokens // (PARTS // 2), width), low.dtype),
            pltpu.VMEM(weight_out.shape, weight_out.dtype),
            pltpu.SemaphoreType.DMA((PARTS + 1,)),
        ],
        name="finish",
        compiler_params=pltpu.CompilerParams(vmem_limit_bytes=20 << 20),
    )(mine, low, high)


def local(normed, w_value, grad_value, assistant_mask):
    inputs = normed[0]
    weight = w_value[0]
    upstream = grad_value[0]
    n = lax.axis_size("dp")
    chips = n // 2
    rows = -(-inputs.shape[1] // n)
    core = lax.rem(lax.axis_index("dp"), 2).reshape(1)

    own, grad, other, low, high = front(core, assistant_mask[0], inputs, upstream, weight, chips, rows)
    partner = lax.ppermute(other, "dp", [(i, i ^ 1) for i in range(n)])
    low, high = (from_behind(half, "pipe", -1) for half in (low, high))
    term = terms(partner, own_terms(own, grad, chips * (rows + 1)))
    parity = [[2 * z + c for z in range(chips)] for c in range(2)]
    mine = lax.psum_scatter(term, "dp", scatter_dimension=0, tiled=True, axis_index_groups=parity)
    weight_grad, input_grad = finish(mine, low, high)
    return (weight_grad.reshape(1, 1, rows, -1), input_grad[None])


def solution(mesh):
    return jax.shard_map(
        local,
        mesh=mesh,
        in_specs=(
            P("pipe", "dp", "tensor"),
            P("pipe", "tensor", None),
            P("pipe", "dp", None),
            P("dp", None, None),
        ),
        out_specs=(P("pipe", "tensor", "dp", None), P("pipe", "dp", "tensor")),
        check_vma=False,
    )
```

```python
import functools

import jax
import jax.numpy as jnp
from jax import lax
from jax.experimental import pallas as pl
from jax.experimental.pallas import tpu as pltpu
from jax.sharding import PartitionSpec as P

DIGITS = 6
EXTRA = 16
TILE = 256
PARTS = 4
VM = pl.BlockSpec(memory_space=pltpu.VMEM)
ANY = pl.BlockSpec(memory_space=pl.ANY)


def from_behind(block, axis, distance):
    devices = range(lax.axis_size(axis))
    route = [(i - distance, i) for i in devices if i - distance in devices]
    return lax.ppermute(block, axis, route)


def front_kernel(
    chips, rows, core_ref, mask_ref, normed_ref, grad_ref, weight_ref, own_ref, grad, other_ref, low_ref, high_ref,
    mask, normed, weight, packs, made, arrived, left,
):
    tokens, width = normed.shape
    lanes, columns = own_ref.shape[1], grad_ref.shape[1]
    step, slab = tokens // PARTS, width // PARTS
    loads = [
        pltpu.make_async_copy(grad_ref, grad.at[pl.ds(0, tokens)], arrived.at[0]),
        pltpu.make_async_copy(mask_ref, mask, arrived.at[1]),
    ]
    for i in range(PARTS):
        at = pl.ds(i * step, step)
        loads.append(pltpu.make_async_copy(weight_ref.at[pl.ds(i * slab, slab)], weight.at[i], arrived.at[2 * i + 2]))
        loads.append(pltpu.make_async_copy(normed_ref.at[at], normed.at[at], arrived.at[2 * i + 3]))
    for load in loads:
        load.start()

    at = lax.broadcasted_iota(jnp.int32, (EXTRA, lanes), 1)
    first = lax.broadcasted_iota(jnp.int32, (EXTRA, lanes), 0) == 0
    marks = first & (at % (rows + 1) == rows) & (at < chips * (rows + 1))
    marks = jnp.where(marks, 1.0, 0.0).astype(jnp.bfloat16)
    for parity in range(2):
        packs[parity, tokens:, :] = marks
    lane = lax.broadcasted_iota(jnp.int32, (EXTRA, columns), 1)
    row = lax.broadcasted_iota(jnp.int32, (EXTRA, columns), 0)
    loads[0].wait()
    loads[1].wait()
    count = jnp.sum(mask[...])
    digit = jnp.bitwise_and(jnp.right_shift(count, 3 * jnp.minimum(lane, DIGITS)), 7)
    digit = jnp.where((lane < DIGITS) & (row == 0), digit, 0).astype(jnp.float32).astype(jnp.bfloat16)
    grad[tokens:, :] = digit
    core = core_ref[0]
    stores = [pltpu.make_async_copy(grad, other_ref.at[:, pl.ds(lanes, columns)], left.at[0])]
    stores[0].start()

    for i in range(PARTS):
        loads[2 * i + 2].wait()
        loads[2 * i + 3].wait()
        made[i] = lax.dot_general(
            grad[:tokens, :], weight[i], (((1,), (1,)), ((), ())), preferred_element_type=jnp.float32
        ).astype(jnp.bfloat16)
        for parity in range(2):
            pieces = []
            for j in range(chips):
                begin = (2 * j + parity) * rows
                end = min(begin + rows, width)
                pieces.append(normed[i * step : (i + 1) * step, begin:end])
                pieces.append(jnp.zeros((step, rows + 1 - (end - begin)), jnp.bfloat16))
            pieces.append(jnp.zeros((step, lanes - chips * (rows + 1)), jnp.bfloat16))
            packs[parity, i * step : (i + 1) * step, :] = jnp.concatenate(pieces, axis=1)
        at = pl.ds(i * step, step if i < PARTS - 1 else step + EXTRA)
        half = (low_ref, high_ref)[2 * i // PARTS]
        place = pl.ds(i % (PARTS // 2) * slab, slab)
        stores.append(pltpu.make_async_copy(made.at[i], half.at[:, place], left.at[3 * i + 1]))
        stores.append(pltpu.make_async_copy(packs.at[1 - core, at], other_ref.at[at, pl.ds(0, lanes)], left.at[3 * i + 2]))
        stores.append(pltpu.make_async_copy(packs.at[core, at], own_ref.at[at], left.at[3 * i + 3]))
        for store in stores[-3:]:
            store.start()
    for store in stores:
        store.wait()


def front(core, mask, inputs, upstream, weight, chips, rows):
    lanes = -(-chips * (rows + 1) // 128) * 128
    (tokens, width), columns = inputs.shape, upstream.shape[1]
    height = tokens + EXTRA
    bf16 = jnp.bfloat16
    half = pltpu.HBM((tokens, width // 2), bf16)
    return pl.pallas_call(
        functools.partial(front_kernel, chips, rows),
        out_shape=(
            pltpu.VMEM((height, lanes), bf16),
            pltpu.VMEM((height, columns), bf16),
            pltpu.VMEM((height, lanes + columns), bf16),
            half,
            half,
        ),
        in_specs=[pl.BlockSpec(memory_space=pltpu.SMEM)] + [pl.BlockSpec(memory_space=pltpu.HBM)] * 4,
        out_specs=(VM,) * 3 + (pl.BlockSpec(memory_space=pltpu.HBM),) * 2,
        scratch_shapes=[
            pltpu.VMEM(mask.shape, mask.dtype),
            pltpu.VMEM(inputs.shape, bf16),
            pltpu.VMEM((PARTS, width // PARTS, columns), bf16),
            pltpu.VMEM((2, height, lanes), bf16),
            pltpu.VMEM((PARTS, tokens, width // PARTS), bf16),
            pltpu.SemaphoreType.DMA((2 * PARTS + 2,)),
            pltpu.SemaphoreType.DMA((3 * PARTS + 1,)),
        ],
        name="front",
        compiler_params=pltpu.CompilerParams(vmem_limit_bytes=40 << 20),
        cost_estimate=pl.CostEstimate(flops=2 * upstream.size * width, bytes_accessed=14 << 20, transcendentals=0),
    )(core, mask, inputs, upstream, weight)


def product(left, right):
    return lax.dot_general(left, right, (((0,), (0,)), ((), ())), preferred_element_type=jnp.float32)


def own_kernel(own_ref, grad_ref, out_ref):
    for m in range(0, out_ref.shape[0], TILE):
        size = min(TILE, out_ref.shape[0] - m)
        out_ref[m : m + size, :] = product(own_ref[:, m : m + size], grad_ref[...])


def own_terms(own, grad, rows):
    width = grad.shape[1]
    return pl.pallas_call(
        own_kernel,
        out_shape=jax.ShapeDtypeStruct((rows, width), jnp.float32),
        in_specs=[VM] * 2,
        out_specs=VM,
        name="own_terms",
        compiler_params=pltpu.CompilerParams(vmem_limit_bytes=20 << 20),
        cost_estimate=pl.CostEstimate(flops=2 * own.shape[0] * rows * width, bytes_accessed=6 << 20, transcendentals=0),
    )(own, grad)


def term_kernel(partner_ref, first_ref, out_ref):
    lanes = partner_ref.shape[1] - out_ref.shape[1]
    for m in range(0, out_ref.shape[0], TILE):
        size = min(TILE, out_ref.shape[0] - m)
        tile = product(partner_ref[:, m : m + size], partner_ref[:, lanes:]) + first_ref[m : m + size, :]
        out_ref[m : m + size, :] = tile.astype(out_ref.dtype)


def terms(partner, first):
    rows, width = first.shape
    return pl.pallas_call(
        term_kernel,
        out_shape=jax.ShapeDtypeStruct((rows, width), jnp.bfloat16),
        in_specs=[VM] * 2,
        out_specs=VM,
        name="terms",
        compiler_params=pltpu.CompilerParams(vmem_limit_bytes=20 << 20),
        cost_estimate=pl.CostEstimate(
            flops=2 * partner.shape[0] * rows * width, bytes_accessed=8 << 20, transcendentals=0
        ),
    )(partner, first)


def finish_kernel(
    mine_ref, low_ref, high_ref, weight_out_ref, passed_out_ref, high, passed, weight_out, arrived, left
):
    rows = weight_out_ref.shape[0]
    width = low_ref.shape[1]
    step = low_ref.shape[0] // (PARTS // 2)
    load = pltpu.make_async_copy(high_ref, high, arrived)
    load.start()
    digits = mine_ref[rows : rows + 1, :128].astype(jnp.float32)
    lane = lax.broadcasted_iota(jnp.int32, (1, 128), 1)
    scale = jnp.where(lane < DIGITS, jnp.left_shift(1, 3 * jnp.minimum(lane, DIGITS)), 0).astype(jnp.float32)
    inverse = 1.0 / jnp.sum(digits * scale)
    stores = []
    for i in range(PARTS):
        half, low = divmod(i, PARTS // 2)
        low *= step
        if half and not low:
            load.wait()
        passed[i] = ((low_ref, high)[half][low : low + step, :].astype(jnp.float32) * inverse).astype(jnp.bfloat16)
        place = passed_out_ref.at[pl.ds(low, step), pl.ds(half * width, width)]
        stores.append(pltpu.make_async_copy(passed.at[i], place, left.at[i]))
        stores[-1].start()
    for q in range(weight_out_ref.shape[1]):
        weight_out[:, q, :] = mine_ref[:rows, 128 * q : 128 * (q + 1)].astype(jnp.float32) * inverse
    stores.append(pltpu.make_async_copy(weight_out, weight_out_ref, left.at[PARTS]))
    stores[-1].start()
    for store in stores:
        store.wait()


def finish(mine, low, high):
    weight_out = jax.ShapeDtypeStruct((mine.shape[0] - 1, mine.shape[1] // 128, 128), jnp.float32)
    tokens, width = low.shape
    return pl.pallas_call(
        finish_kernel,
        out_shape=(weight_out, jax.ShapeDtypeStruct((tokens, 2 * width), low.dtype)),
        in_specs=[VM, VM, ANY],
        out_specs=(ANY, ANY),
        scratch_shapes=[
            pltpu.VMEM(high.shape, high.dtype),
            pltpu.VMEM((PARTS, tokens // (PARTS // 2), width), low.dtype),
            pltpu.VMEM(weight_out.shape, weight_out.dtype),
            pltpu.SemaphoreType.DMA,
            pltpu.SemaphoreType.DMA((PARTS + 1,)),
        ],
        name="finish",
        compiler_params=pltpu.CompilerParams(vmem_limit_bytes=20 << 20),
    )(mine, low, high)


def local(normed, w_value, grad_value, assistant_mask):
    inputs = normed[0]
    weight = w_value[0]
    upstream = grad_value[0]
    n = lax.axis_size("dp")
    chips = n // 2
    rows = -(-inputs.shape[1] // n)
    core = lax.rem(lax.axis_index("dp"), 2).reshape(1)

    operands = (pltpu.with_memory_space_constraint(x, pltpu.HBM) for x in (assistant_mask[0], inputs, upstream, weight))
    own, grad, other, low, high = front(core, *operands, chips, rows)
    partner = lax.ppermute(other, "dp", [(i, i ^ 1) for i in range(n)])
    low, high = (from_behind(half, "pipe", -1) for half in (low, high))
    term = terms(partner, own_terms(own, grad, chips * (rows + 1)))
    parity = [[2 * z + c for z in range(chips)] for c in range(2)]
    mine = lax.psum_scatter(term, "dp", scatter_dimension=0, tiled=True, axis_index_groups=parity)
    weight_grad, input_grad = finish(mine, low, high)
    return (weight_grad.reshape(1, 1, rows, -1), input_grad[None])


def solution(mesh):
    return jax.shard_map(
        local,
        mesh=mesh,
        in_specs=(
            P("pipe", "dp", "tensor"),
            P("pipe", "tensor", None),
            P("pipe", "dp", None),
            P("dp", None, None),
        ),
        out_specs=(P("pipe", "tensor", "dp", None), P("pipe", "dp", "tensor")),
        check_vma=False,
    )
```

```python
import functools

import jax
import jax.numpy as jnp
from jax import lax
from jax.experimental import pallas as pl
from jax.experimental.pallas import tpu as pltpu
from jax.sharding import PartitionSpec as P

DIGITS = 6
EXTRA = 16
TILE = 256
PARTS = 4
VM = pl.BlockSpec(memory_space=pltpu.VMEM)
ANY = pl.BlockSpec(memory_space=pl.ANY)


def from_behind(block, axis, distance):
    devices = range(lax.axis_size(axis))
    route = [(i - distance, i) for i in devices if i - distance in devices]
    return lax.ppermute(block, axis, route)


def front_kernel(
    chips, rows, core_ref, mask_ref, normed_ref, grad_ref, weight_ref, own_ref, own_grad_ref, other_ref, total_ref,
    mask, normed, weight, made, arrived, left,
):
    tokens, width = normed.shape
    lanes, columns = own_ref.shape[1], grad_ref.shape[1]
    step, slab = tokens // PARTS, width // PARTS
    beside = other_ref.at[:, pl.ds(lanes, columns)]
    loads = [
        pltpu.make_async_copy(grad_ref, own_grad_ref.at[pl.ds(0, tokens)], arrived.at[0]),
        pltpu.make_async_copy(mask_ref, mask, arrived.at[1]),
    ]
    for i in range(PARTS):
        at = pl.ds(i * step, step)
        loads.append(pltpu.make_async_copy(weight_ref.at[pl.ds(i * slab, slab)], weight.at[i], arrived.at[2 * i + 2]))
        loads.append(pltpu.make_async_copy(normed_ref.at[at], normed.at[at], arrived.at[2 * i + 3]))
    loads.append(pltpu.make_async_copy(grad_ref, beside.at[pl.ds(0, tokens)], arrived.at[2 * PARTS + 2]))
    for load in loads:
        load.start()

    at = lax.broadcasted_iota(jnp.int32, (EXTRA, lanes), 1)
    first = lax.broadcasted_iota(jnp.int32, (EXTRA, lanes), 0) == 0
    marks = first & (at % (rows + 1) == rows) & (at < chips * (rows + 1))
    marks = jnp.where(marks, 1.0, 0.0).astype(jnp.bfloat16)
    own_ref[tokens:, :] = marks
    other_ref[tokens:, :lanes] = marks
    lane = lax.broadcasted_iota(jnp.int32, (EXTRA, columns), 1)
    row = lax.broadcasted_iota(jnp.int32, (EXTRA, columns), 0)
    loads[1].wait()
    count = jnp.sum(mask[...])
    digit = jnp.bitwise_and(jnp.right_shift(count, 3 * jnp.minimum(lane, DIGITS)), 7)
    digit = jnp.where((lane < DIGITS) & (row == 0), digit, 0).astype(jnp.float32).astype(jnp.bfloat16)
    own_grad_ref[tokens:, :] = digit
    other_ref[tokens:, lanes:] = digit
    even = core_ref[0] == 0
    loads[0].wait()

    stores = []
    for i in range(PARTS):
        loads[2 * i + 2].wait()
        loads[2 * i + 3].wait()
        made[i] = lax.dot_general(
            own_grad_ref[:tokens, :], weight[i], (((1,), (1,)), ((), ())), preferred_element_type=jnp.float32
        ).astype(jnp.bfloat16)
        packs = []
        for parity in range(2):
            pieces = []
            for j in range(chips):
                begin = (2 * j + parity) * rows
                end = min(begin + rows, width)
                pieces.append(normed[i * step : (i + 1) * step, begin:end])
                pieces.append(jnp.zeros((step, rows + 1 - (end - begin)), jnp.bfloat16))
            pieces.append(jnp.zeros((step, lanes - chips * (rows + 1)), jnp.bfloat16))
            packs.append(jnp.concatenate(pieces, axis=1))
        own_ref[i * step : (i + 1) * step, :] = jnp.where(even, packs[0], packs[1])
        other_ref[i * step : (i + 1) * step, :lanes] = jnp.where(even, packs[1], packs[0])
        stores.append(pltpu.make_async_copy(made.at[i], total_ref.at[:, pl.ds(i * slab, slab)], left.at[i]))
        stores[-1].start()
    loads[-1].wait()
    for store in stores:
        store.wait()


def front(core, mask, inputs, upstream, weight, chips, rows):
    lanes = -(-chips * (rows + 1) // 128) * 128
    (tokens, width), columns = inputs.shape, upstream.shape[1]
    height = tokens + EXTRA
    bf16 = jnp.bfloat16
    hbm = pl.BlockSpec(memory_space=pltpu.HBM)
    return pl.pallas_call(
        functools.partial(front_kernel, chips, rows),
        out_shape=(
            pltpu.VMEM((height, lanes), bf16),
            pltpu.VMEM((height, columns), bf16),
            pltpu.VMEM((height, lanes + columns), bf16),
            pltpu.HBM((tokens, width), bf16),
        ),
        in_specs=[pl.BlockSpec(memory_space=pltpu.SMEM)] + [hbm] * 4,
        out_specs=(VM, VM, VM, hbm),
        scratch_shapes=[
            pltpu.VMEM(mask.shape, mask.dtype),
            pltpu.VMEM(inputs.shape, bf16),
            pltpu.VMEM((PARTS, width // PARTS, columns), bf16),
            pltpu.VMEM((PARTS, tokens, width // PARTS), bf16),
            pltpu.SemaphoreType.DMA((2 * PARTS + 3,)),
            pltpu.SemaphoreType.DMA((PARTS,)),
        ],
        name="front",
        compiler_params=pltpu.CompilerParams(vmem_limit_bytes=40 << 20),
        cost_estimate=pl.CostEstimate(flops=2 * upstream.size * width, bytes_accessed=14 << 20, transcendentals=0),
    )(core, mask, inputs, upstream, weight)


def product(left, right):
    return lax.dot_general(left, right, (((0,), (0,)), ((), ())), preferred_element_type=jnp.float32)


def own_kernel(own_ref, grad_ref, out_ref):
    for m in range(0, out_ref.shape[0], TILE):
        size = min(TILE, out_ref.shape[0] - m)
        out_ref[m : m + size, :] = product(own_ref[:, m : m + size], grad_ref[...])


def own_terms(own, grad, rows):
    width = grad.shape[1]
    return pl.pallas_call(
        own_kernel,
        out_shape=jax.ShapeDtypeStruct((rows, width), jnp.float32),
        in_specs=[VM] * 2,
        out_specs=VM,
        name="own_terms",
        compiler_params=pltpu.CompilerParams(vmem_limit_bytes=20 << 20),
        cost_estimate=pl.CostEstimate(flops=2 * own.shape[0] * rows * width, bytes_accessed=6 << 20, transcendentals=0),
    )(own, grad)


def term_kernel(partner_ref, first_ref, out_ref):
    lanes = partner_ref.shape[1] - out_ref.shape[1]
    for m in range(0, out_ref.shape[0], TILE):
        size = min(TILE, out_ref.shape[0] - m)
        tile = product(partner_ref[:, m : m + size], partner_ref[:, lanes:]) + first_ref[m : m + size, :]
        out_ref[m : m + size, :] = tile.astype(out_ref.dtype)


def terms(partner, first):
    rows, width = first.shape
    return pl.pallas_call(
        term_kernel,
        out_shape=jax.ShapeDtypeStruct((rows, width), jnp.bfloat16),
        in_specs=[VM] * 2,
        out_specs=VM,
        name="terms",
        compiler_params=pltpu.CompilerParams(vmem_limit_bytes=20 << 20),
        cost_estimate=pl.CostEstimate(
            flops=2 * partner.shape[0] * rows * width, bytes_accessed=8 << 20, transcendentals=0
        ),
    )(partner, first)


def finish_kernel(mine_ref, passed_ref, weight_out_ref, passed_out_ref, mine, passed, weight_out, arrived, left):
    rows = weight_out_ref.shape[0]
    parts = PARTS
    step = passed.shape[0] // parts
    loads = [pltpu.make_async_copy(mine_ref, mine, arrived.at[parts])]
    for i in range(parts):
        at = pl.ds(i * step, step)
        loads.append(pltpu.make_async_copy(passed_ref.at[at], passed.at[at], arrived.at[i]))
    for load in loads:
        load.start()
    loads[0].wait()
    digits = mine[rows : rows + 1, :128].astype(jnp.float32)
    lane = lax.broadcasted_iota(jnp.int32, (1, 128), 1)
    scale = jnp.where(lane < DIGITS, jnp.left_shift(1, 3 * jnp.minimum(lane, DIGITS)), 0).astype(jnp.float32)
    inverse = 1.0 / jnp.sum(digits * scale)
    for q in range(weight_out_ref.shape[1]):
        weight_out[:, q, :] = mine[:rows, 128 * q : 128 * (q + 1)].astype(jnp.float32) * inverse
    stores = [pltpu.make_async_copy(weight_out, weight_out_ref, left.at[parts])]
    stores[0].start()
    for i in range(parts):
        at = pl.ds(i * step, step)
        loads[i + 1].wait()
        passed[at, :] = (passed[at, :].astype(jnp.float32) * inverse).astype(jnp.bfloat16)
        stores.append(pltpu.make_async_copy(passed.at[at], passed_out_ref.at[at], left.at[i]))
        stores[-1].start()
    for store in stores:
        store.wait()


def finish(mine, passed):
    weight_out = jax.ShapeDtypeStruct((mine.shape[0] - 1, mine.shape[1] // 128, 128), jnp.float32)
    return pl.pallas_call(
        finish_kernel,
        out_shape=(weight_out, jax.ShapeDtypeStruct(passed.shape, jnp.bfloat16)),
        in_specs=[ANY, ANY],
        out_specs=(ANY, ANY),
        scratch_shapes=[
            pltpu.VMEM(mine.shape, mine.dtype),
            pltpu.VMEM(passed.shape, passed.dtype),
            pltpu.VMEM(weight_out.shape, weight_out.dtype),
            pltpu.SemaphoreType.DMA((PARTS + 1,)),
            pltpu.SemaphoreType.DMA((PARTS + 1,)),
        ],
        name="finish",
        compiler_params=pltpu.CompilerParams(vmem_limit_bytes=20 << 20),
    )(mine, passed)


def local(normed, w_value, grad_value, assistant_mask):
    inputs = normed[0]
    weight = w_value[0]
    upstream = grad_value[0]
    n = lax.axis_size("dp")
    chips = n // 2
    rows = -(-inputs.shape[1] // n)
    core = lax.rem(lax.axis_index("dp"), 2).reshape(1)

    operands = (pltpu.with_memory_space_constraint(x, pltpu.HBM) for x in (assistant_mask[0], inputs, upstream, weight))
    own, grad, other, total = front(core, *operands, chips, rows)
    partner = lax.ppermute(other, "dp", [(i, i ^ 1) for i in range(n)])
    passed = from_behind(total, "pipe", -1)
    term = terms(partner, own_terms(own, grad, chips * (rows + 1)))
    parity = [[2 * z + c for z in range(chips)] for c in range(2)]
    mine = lax.psum_scatter(term, "dp", scatter_dimension=0, tiled=True, axis_index_groups=parity)
    weight_grad, input_grad = finish(mine, passed)
    return (weight_grad.reshape(1, 1, rows, -1), input_grad[None])


def solution(mesh):
    return jax.shard_map(
        local,
        mesh=mesh,
        in_specs=(
            P("pipe", "dp", "tensor"),
            P("pipe", "tensor", None),
            P("pipe", "dp", None),
            P("dp", None, None),
        ),
        out_specs=(P("pipe", "tensor", "dp", None), P("pipe", "dp", "tensor")),
        check_vma=False,
    )
```
